512 devices in a mesh: grp: 8 (over z), own: 64 (over y, x, core).
Axes of the slice: x: 4, y: 8, z: 8, core: 2. Of those that a mesh axis runs over, the one named last changes fastest.
Arguments:
- amps: bfloat16 [14336, 128, 128], P(('grp', 'own')), may hold values from -0.35 to 0.35, as said below
- ints: bfloat16 [14336, 128, 128], P(('grp', 'own')), may hold values from -0.5 to 0.5, as said below
- pno_energy: float32 [14336, 128], P(('grp', 'own')), may hold values from 0.2 to 2, as said below
- occ_energy: float32 [1000], replicated, may hold values from -1 to -0.2
- pair_occ: int32 [2, 14336], P(None, ('grp', 'own')), may hold values from 0 to 999, as said below
- mirror: int32 [14336], P(('grp', 'own')), may hold values from 0 to 14335, as said below
- edge_src: int32 [24576], P(('grp', 'own')), may hold values from 0 to 14335, as said below
- edge_dst: int32 [24576], P('grp'), may hold values from 0 to 14335, as said below
- edge_fock: float32 [24576], P(('grp', 'own')), may hold values from -6 to 6
- margin: bfloat16 [24576, 128, 128], P(('grp', 'own')), may hold values from -0.15 to 1.15
Outputs:
- residual: bfloat16 [14336, 128, 128], P(('grp', 'own'))
The draws below stay inside these ranges and needn't reach their ends.
Inputs may be any that keep to these rules, and one draw needn't show every extreme that they name: `pair_occ`: each pair's two indices differ. The pair at mirror[p] has its two indices swapped. mirror is an involution without fixed points; a pair and its mirror lie in the same grp block of pairs but never on the same device; amps and ints of mirror[p] are the transposes of those of p, and pno_energy is equal. Of one device's pairs at most 1 have their mirror on any one other device, and that many do for some device. `edge_src`: every edge of a device has its source pair on that same device. `edge_dst`: an edge's target pair lies in the same group as its source, on another device; of one device's edges at most 1 end on pairs of any one other device, and at most 1 have the mirror of their target pair on any one device (that device itself included); both bounds are reached on some device. `amps`: mirror pairs hold transposed tiles. `ints`: mirror pairs hold transposed tiles. `pno_energy`: mirror pairs hold equal rows.
All inputs are finite; a program needn't handle non-finite values.
Results may differ from the reference program's by a relative error of at most 0.0065.
Values may be sent and summed in bfloat16 or wider, within the bound.
No kernel may reach another device: no remote copies, remote signals or barrier semaphores. Data moves between devices by JAX's collectives and lax.ppermute only.
A program may use at most 64 MiB of HBM per device.

```python
import jax
import jax.numpy as jnp
from jax import lax

RANK = 128
NOCC = 1000
PAIR_DEV = 28
EDGE_DEV = 48
PAIRS = 14336
EDGES = 24576
N_GRP = 8
N_OWN = 64


def owner_labels(key):
    labels = jax.vmap(lambda sub_key: jax.random.permutation(sub_key, N_OWN))(jax.random.split(key, N_GRP)).astype(jnp.int32)
    inverse = jnp.argsort(labels, axis=1).astype(jnp.int32)
    values = jax.vmap(lambda sub_key: jax.random.permutation(sub_key, N_OWN - 1))(jax.random.split(jax.random.fold_in(key, 5), N_GRP)).astype(jnp.int32) + 1
    return (labels, inverse, values)


def couple_structure(key):
    labels, inverse, values = owner_labels(jax.random.fold_in(key, 1))
    rounds = jnp.arange(PAIR_DEV) % (N_OWN - 1)
    xor_round = values[:, rounds]
    partner_label = jnp.bitwise_xor(labels[:, :, None], xor_round[:, None, :])
    partner = jax.vmap(lambda inverse_row, label_row: inverse_row[label_row])(inverse, partner_label)
    leader = labels[:, :, None] < partner_label
    slot_keys = jax.random.split(jax.random.fold_in(key, 2), N_GRP * N_OWN)
    slot_round = jax.vmap(lambda sub_key: jax.random.permutation(sub_key, PAIR_DEV))(slot_keys).astype(jnp.int32).reshape(N_GRP, N_OWN, PAIR_DEV)
    round_slot = jnp.argsort(slot_round, axis=2).astype(jnp.int32)
    groups = jnp.arange(N_GRP, dtype=jnp.int32)[:, None, None]
    owners = jnp.arange(N_OWN, dtype=jnp.int32)[None, :, None]
    part_at = jnp.take_along_axis(partner, slot_round, axis=2)
    lead_at = jnp.take_along_axis(leader, slot_round, axis=2)
    mirror_slot = round_slot[groups, part_at, slot_round]
    mirror = (groups * N_OWN + part_at) * PAIR_DEV + mirror_slot
    lead_owner = jnp.where(lead_at, owners, part_at)
    content = (groups * N_OWN + lead_owner) * PAIR_DEV + slot_round
    return (mirror.reshape(-1).astype(jnp.int32), lead_at.reshape(-1), content.reshape(-1).astype(jnp.int32), labels, inverse, values, round_slot)


def couple_layout(key):
    mirror, lead_flag, content, labels, inverse, values, round_slot = couple_structure(key)
    return (mirror, lead_flag, content)


def couple_tiles(key, base_table):
    mirror, lead_flag, content = couple_layout(jax.random.fold_in(key, 101))
    picked = base_table[content]
    return jnp.where(lead_flag[:, None, None], picked, jnp.swapaxes(picked, 1, 2))


def draw_amps(key, part):
    jitter = jax.random.normal(jax.random.fold_in(key, 7), (PAIRS, RANK, RANK), jnp.float32)
    base_table = jnp.clip(0.07 * jitter, -0.35, 0.35)
    return couple_tiles(key, base_table).astype(jnp.bfloat16)


def draw_ints(key, part):
    jitter = jax.random.normal(jax.random.fold_in(key, 8), (PAIRS, RANK, RANK), jnp.float32)
    base_table = jnp.clip(0.1 * jitter, -0.5, 0.5)
    return couple_tiles(key, base_table).astype(jnp.bfloat16)


def draw_pno_energy(key, part):
    mirror, lead_flag, content = couple_layout(jax.random.fold_in(key, 101))
    base_table = jax.random.uniform(jax.random.fold_in(key, 12), (PAIRS, RANK), jnp.float32, 0.2, 2.0)
    return base_table[content]


def draw_pair_occ(key, part):
    mirror, lead_flag, content = couple_layout(jax.random.fold_in(key, 101))
    first_occ = jax.random.randint(jax.random.fold_in(key, 9), (PAIRS,), 0, NOCC)
    offset = jax.random.randint(jax.random.fold_in(key, 10), (PAIRS,), 1, NOCC)
    second_occ = (first_occ + offset) % NOCC
    first_moved = first_occ[content]
    second_moved = second_occ[content]
    occ_left = jnp.where(lead_flag, first_moved, second_moved)
    occ_right = jnp.where(lead_flag, second_moved, first_moved)
    return jnp.stack([occ_left, occ_right]).astype(jnp.int32)


def draw_mirror(key, part):
    mirror, lead_flag, content = couple_layout(jax.random.fold_in(key, 101))
    return mirror


def edge_layout(key):
    mirror, lead_flag, content, labels, inverse, values, round_slot = couple_structure(jax.random.fold_in(key, 101))
    edge_key = jax.random.fold_in(key, 202)
    order_keys = jax.random.split(jax.random.fold_in(edge_key, 3), N_GRP * N_OWN)
    order = jax.vmap(lambda sub_key: jax.random.permutation(sub_key, N_OWN - 1))(order_keys).astype(jnp.int32).reshape(N_GRP, N_OWN, N_OWN - 1)
    own_round = jax.random.randint(jax.random.fold_in(edge_key, 4), (N_GRP, N_OWN), 0, PAIR_DEV).astype(jnp.int32)
    shift_val = jnp.take_along_axis(values, own_round % (N_OWN - 1), axis=1)
    cycle_pos = jnp.arange(EDGE_DEV) % (N_OWN - 1)
    picked = order[:, :, cycle_pos]
    offset = picked + (picked >= shift_val[:, :, None]).astype(jnp.int32)
    target_label = jnp.bitwise_xor(jnp.bitwise_xor(labels[:, :, None], offset), shift_val[:, :, None])
    target_owner = jax.vmap(lambda inverse_row, label_row: inverse_row[label_row])(inverse, target_label)
    groups = jnp.arange(N_GRP, dtype=jnp.int32)[:, None, None]
    owners = jnp.arange(N_OWN, dtype=jnp.int32)[None, :, None]
    target_slot = round_slot[groups, target_owner, own_round[:, :, None]]
    source_slot = jax.random.randint(jax.random.fold_in(edge_key, 6), (N_GRP, N_OWN, EDGE_DEV), 0, PAIR_DEV).astype(jnp.int32)
    target = (groups * N_OWN + target_owner) * PAIR_DEV + target_slot
    source = (groups * N_OWN + owners) * PAIR_DEV + source_slot
    return (source.reshape(-1).astype(jnp.int32), target.reshape(-1).astype(jnp.int32))


def draw_edge_src(key, part):
    source, target = edge_layout(key)
    return source


def draw_edge_dst(key, part):
    source, target = edge_layout(key)
    return target


def draw_margin(key, part):
    diag_part = jax.random.uniform(jax.random.fold_in(key, 21), (EDGES, RANK), jnp.float32, 0.6, 1.0)
    jitter = jax.random.normal(jax.random.fold_in(key, 22), (EDGES, RANK, RANK), jnp.float32) * 0.03
    jitter = jnp.clip(jitter, -0.12, 0.12)
    return (jitter + diag_part[:, :, None] * jnp.eye(RANK, dtype=jnp.float32)[None]).astype(jnp.bfloat16)


def shard_levels(stream_key, extent, cuts, low, high):
    def one(axis_at, blocks):
        heights = jax.random.uniform(jax.random.fold_in(jax.random.fold_in(stream_key, 6), axis_at), (blocks,), jnp.float32, low / len(cuts), high / len(cuts))
        return jnp.repeat(jnp.exp(heights), extent[axis_at] // blocks).reshape((-1,) + (1,) * (len(extent) - axis_at - 1))

    loudness = one(*cuts[0])
    for cut in cuts[1:]:
        loudness = loudness * one(*cut)
    return loudness


def setup_inputs(seed: int = 0) -> dict:
    splits = jax.random.split(jax.random.key(seed), 11)
    amps = draw_amps(jax.random.fold_in(splits[10], 71), 0)
    ints = draw_ints(jax.random.fold_in(splits[10], 71), 0)
    pno_energy = draw_pno_energy(jax.random.fold_in(splits[10], 71), 0)
    occ_energy = jnp.clip(jax.random.uniform(splits[3], (NOCC,), jnp.float32, -1.0, -0.2), -1.0, -0.2)
    pair_occ = draw_pair_occ(jax.random.fold_in(splits[10], 71), 0)
    mirror = draw_mirror(jax.random.fold_in(splits[10], 71), 0)
    edge_src = draw_edge_src(jax.random.fold_in(splits[10], 71), 0)
    edge_dst = draw_edge_dst(jax.random.fold_in(splits[10], 71), 0)
    edge_fock = jnp.clip(jax.random.uniform(splits[8], (EDGES,), jnp.float32, -6.0, 6.0) * shard_levels(splits[8], (EDGES,), ((0, 512),), -0.4, 0.0), -6.0, 6.0)
    margin = draw_margin(jax.random.fold_in(splits[10], 71), 0)
    return {"amps": amps, "ints": ints, "pno_energy": pno_energy, "occ_energy": occ_energy, "pair_occ": pair_occ, "mirror": mirror, "edge_src": edge_src, "edge_dst": edge_dst, "edge_fock": edge_fock, "margin": margin}


def reference(amps, ints, pno_energy, occ_energy, pair_occ, mirror, edge_src, edge_dst, edge_fock, margin):
    amp_f32 = amps.astype(jnp.float32)
    int_f32 = ints.astype(jnp.float32)
    pair_energy = jnp.sum((2.0 * int_f32 - jnp.swapaxes(int_f32, 1, 2)) * amp_f32, axis=(1, 2))
    first_occ = pair_occ[0].astype(jnp.int32)
    second_occ = pair_occ[1].astype(jnp.int32)
    occ_sum = jnp.zeros((NOCC,), jnp.float32).at[first_occ].add(pair_energy)
    cepa_shift = 0.5 * (occ_sum[first_occ] + occ_sum[second_occ])
    fock_pair = occ_energy[first_occ] + occ_energy[second_occ]
    diagonal = (pno_energy[:, :, None] + pno_energy[:, None, :] - fock_pair[:, None, None]) - cepa_shift[:, None, None]
    local_part = 0.5 * int_f32 + diagonal * amp_f32

    blocks = EDGES // EDGE_DEV

    def project(inputs):
        source_ids, margin_block, fock_row = inputs
        source_tiles = jnp.take(amps, source_ids, axis=0).astype(jnp.float32)
        margin_f32 = margin_block.astype(jnp.float32)
        projected = jnp.einsum("eab,ebc->eac", margin_f32, source_tiles).astype(jnp.bfloat16)
        product = jnp.einsum("eab,ecb->eac", projected.astype(jnp.float32), margin_f32)
        return (product * fock_row[:, None, None]).astype(jnp.bfloat16)

    coupled = lax.map(project, (edge_src.reshape(blocks, EDGE_DEV), margin.reshape(blocks, EDGE_DEV, RANK, RANK), edge_fock.reshape(blocks, EDGE_DEV)))
    coupled = coupled.reshape(EDGES, RANK, RANK)
    coupling = jnp.zeros((PAIRS, RANK, RANK), jnp.float32).at[edge_dst].add(coupled.astype(jnp.float32))
    half_res = (local_part + coupling).astype(jnp.bfloat16)
    partner = jnp.swapaxes(jnp.take(half_res, mirror, axis=0), 1, 2)
    return (half_res.astype(jnp.float32) + partner.astype(jnp.float32)).astype(jnp.bfloat16)
```

```python
import jax
import jax.numpy as jnp
from jax import lax
from jax.experimental import pallas as pl
from jax.experimental.pallas import tpu as pltpu
from jax.sharding import PartitionSpec as P

LANES = 128
F32 = jnp.float32
BF16 = jnp.bfloat16


def contract_last(left, right):
    return lax.dot_general(left, right, (((1,), (1,)), ((), ())), preferred_element_type=F32)


def project_kernel(src_ref, margin_ref, amps_ref, out_ref):
    step = pl.program_id(0)
    count = margin_ref.shape[0]
    for k in range(count):
        tile = amps_ref[src_ref[step * count + k]]
        out_ref[k] = jnp.dot(margin_ref[k], tile, preferred_element_type=F32).astype(BF16)


def energy_kernel(amps_ref, ints_ref, out_ref):
    for k in range(amps_ref.shape[0]):
        amp = amps_ref[k].astype(F32)
        integral = ints_ref[k].astype(F32)
        out_ref[k] = jnp.sum((2.0 * integral - integral.T) * amp, axis=0, keepdims=True)


def couple_kernel(table_ref, place_ref, owner_ref, fock_ref, proj_ref, margin_ref, out_ref):
    step = pl.program_id(0)
    count = margin_ref.shape[0]
    half = margin_ref.shape[1] // 2
    for k in range(count):
        e = step * count + k
        code = table_ref[place_ref[e]]
        lead = (code & 1) == 1
        other = code >> 1
        proj = proj_ref[k]
        marg = margin_ref[k]
        turned = jnp.concatenate([marg[half:], marg[:half]], axis=0)
        left = jnp.where(lead, proj, turned)
        right = jnp.where(lead, marg, proj)
        tile = (contract_last(left, right) * fock_ref[e]).astype(BF16)
        out_ref[owner_ref[e], :half, :] = tile[:half]
        out_ref[other, half:, :] = tile[half:]


def base_kernel(lead_ref, occ_ref, first_ref, second_ref, amps_ref, ints_ref, pno_ref, base_ref, amp_ref):
    step = pl.program_id(0)
    count = amps_ref.shape[0]
    half = amps_ref.shape[1] // 2
    for k in range(count):
        p = step * count + k
        fock = occ_ref[first_ref[p]] + occ_ref[second_ref[p]]
        row = jnp.broadcast_to(pno_ref[k], (2 * half, 2 * half))
        level = row + row.T - fock

        @pl.when(lead_ref[p] == 1)
        def _():
            amp = amps_ref[k][:half]
            base_ref[k] = 0.5 * ints_ref[k][:half].astype(F32) + level[:half] * amp.astype(F32)
            amp_ref[k] = amp

        @pl.when(lead_ref[p] == 0)
        def _():
            amp = amps_ref[k].astype(F32).T[half:]
            integral = ints_ref[k].astype(F32).T[half:]
            base_ref[k] = 0.5 * integral + level[half:] * amp
            amp_ref[k] = amp.astype(BF16)


def sum_kernel(direct_ref, turned_ref, target_ref, shift_ref, arrived_ref, base_ref, amp_ref, sent_ref, own_ref, direct_acc, turned_acc):
    step = pl.program_id(0)
    count = arrived_ref.shape[0]
    half = arrived_ref.shape[1] // 2
    pairs = own_ref.shape[0]

    @pl.when(step == 0)
    def _():
        direct_acc[...] = jnp.zeros_like(direct_acc)
        turned_acc[...] = jnp.zeros_like(turned_acc)

    for k in range(count):
        s = step * count + k
        direct_acc[direct_ref[s]] += arrived_ref[k, :half, :].astype(F32)
        turned_acc[turned_ref[s]] += arrived_ref[k, half:, :].astype(F32)

    @pl.when(step == pl.num_programs(0) - 1)
    def _():
        def finish(p, carry):
            local = base_ref[p] - shift_ref[p] * amp_ref[p].astype(F32)
            first = (local + direct_acc[p]).astype(BF16)
            second = (local + turned_acc[p]).astype(BF16)
            res = (first.astype(F32) + second.astype(F32)).astype(BF16)
            own_ref[p] = res
            sent_ref[target_ref[p]] = res
            return carry

        lax.fori_loop(0, pairs, finish, 0, unroll=2)


def join_kernel(lead_ref, target_ref, returned_ref, own_ref, out_ref):
    step = pl.program_id(0)
    count = out_ref.shape[0]
    half = own_ref.shape[1]
    for k in range(count):
        p = step * count + k

        @pl.when(lead_ref[p] == 1)
        def _():
            out_ref[k, :half, :] = own_ref[k]
            out_ref[k, half:, :] = returned_ref[target_ref[p]]

        @pl.when(lead_ref[p] == 0)
        def _():
            whole = jnp.concatenate([returned_ref[target_ref[p]], own_ref[k]], axis=0)
            out_ref[k] = whole.astype(F32).T.astype(BF16)


def blocks(count, *rest):
    zeros = (0,) * len(rest)
    return pl.BlockSpec((count, *rest), lambda i, *_: (i, *zeros))


def whole(*shape):
    zeros = (0,) * len(shape)
    return pl.BlockSpec(shape, lambda i, *_: zeros)


def call(kernel, name, prefetch, grid, in_specs, out_specs, out_shape, flops, nbytes, scratch=()):
    return pl.pallas_call(
        kernel,
        grid_spec=pltpu.PrefetchScalarGridSpec(
            num_scalar_prefetch=prefetch,
            grid=(grid,),
            in_specs=in_specs,
            out_specs=out_specs,
            scratch_shapes=scratch,
        ),
        out_shape=out_shape,
        name=name,
        cost_estimate=pl.CostEstimate(flops=flops, bytes_accessed=nbytes, transcendentals=0),
        compiler_params=pltpu.CompilerParams(dimension_semantics=("arbitrary",)),
    )


def pick_rows(lookup, hit_mask):
    return jnp.sum(jnp.where(hit_mask, lookup[None, :], 0.0), axis=1)


def all_sum(value, axis, size):
    step = 1
    while step < size:
        value = value + lax.ppermute(value, axis, [(i, i ^ step) for i in range(size)])
        step *= 2
    return value


def exchange(tiles):
    return lax.all_to_all(tiles, "own", split_axis=0, concat_axis=0, tiled=True)


def local(
    amps, ints, pno_energy, occ_energy, pair_occ, mirror, edge_src, edge_dst, edge_fock, margin
):
    owners = lax.axis_size("own")
    groups = lax.axis_size("grp")
    my_owner = lax.axis_index("own")
    group_index = lax.axis_index("grp")
    pairs, rank, _ = amps.shape
    half = rank // 2
    edges = edge_src.shape[0]
    occ_count = occ_energy.shape[0]
    group_base = group_index * (owners * pairs)
    device_base = group_base + my_owner * pairs
    tile_bytes = rank * rank * 2

    ids = device_base + lax.iota(jnp.int32, pairs)
    lead = (ids < mirror).astype(jnp.int32)
    mirror_owner = (mirror - group_base) // pairs
    code = jnp.pad(mirror_owner * 2 + lead, (0, LANES - pairs))
    codes = exchange(jnp.broadcast_to(code[None, None, :], (owners, 1, LANES)))
    table = codes.reshape(owners * LANES)

    edge_step = 8
    projected = call(
        project_kernel,
        "project",
        1,
        edges // edge_step,
        [blocks(edge_step, rank, rank), whole(pairs, rank, rank)],
        blocks(edge_step, rank, rank),
        jax.ShapeDtypeStruct((edges, rank, rank), BF16),
        2 * edges * rank**3,
        (2 * edges + pairs) * tile_bytes,
    )(edge_src - device_base, margin, amps)

    pair_step = 4
    lane_energy = call(
        energy_kernel,
        "energy",
        0,
        pairs // pair_step,
        [blocks(pair_step, rank, rank), blocks(pair_step, rank, rank)],
        blocks(pair_step, 1, rank),
        jax.ShapeDtypeStruct((pairs, 1, rank), F32),
        6 * pairs * rank**2,
        2 * pairs * tile_bytes,
    )(amps, ints)
    pair_energy = jnp.sum(lane_energy, axis=(1, 2))
    padded = -(-occ_count // LANES) * LANES
    occ_ids = lax.iota(jnp.int32, padded)
    first_hit = pair_occ[0][:, None] == occ_ids[None, :]
    second_hit = pair_occ[1][:, None] == occ_ids[None, :]
    partial_value = jnp.sum(jnp.where(first_hit, pair_energy[:, None], 0.0), axis=0)

    group_dst = edge_dst - group_base
    dst_owner = group_dst // pairs
    dst_slot = group_dst % pairs
    my_owner_row = lax.dynamic_slice_in_dim(dst_owner, my_owner * edges, edges)
    my_slot_row = lax.dynamic_slice_in_dim(dst_slot, my_owner * edges, edges)
    outgoing = call(
        couple_kernel,
        "couple",
        4,
        edges // edge_step,
        [blocks(edge_step, rank, rank), blocks(edge_step, rank, rank)],
        whole(owners, rank, rank),
        jax.ShapeDtypeStruct((owners, rank, rank), BF16),
        2 * edges * rank**3,
        (2 * edges + owners) * tile_bytes,
    )(table, my_owner_row * LANES + my_slot_row, my_owner_row, edge_fock, projected, margin)
    arrived = exchange(outgoing)

    total = partial_value.reshape(padded // LANES, LANES)
    total = all_sum(total, "grp", groups)
    total = all_sum(total, "own", owners)
    occ_sums = total.reshape(padded)
    shift = 0.5 * (pick_rows(occ_sums, first_hit) + pick_rows(occ_sums, second_hit))
    base, amp_half = call(
        base_kernel,
        "base",
        4,
        pairs // pair_step,
        [blocks(pair_step, rank, rank), blocks(pair_step, rank, rank), blocks(pair_step, 1, rank)],
        [blocks(pair_step, half, rank), blocks(pair_step, half, rank)],
        [
            jax.ShapeDtypeStruct((pairs, half, rank), F32),
            jax.ShapeDtypeStruct((pairs, half, rank), BF16),
        ],
        6 * pairs * rank**2,
        4 * pairs * tile_bytes,
    )(lead, occ_energy, pair_occ[0], pair_occ[1], amps, ints, pno_energy.reshape(pairs, 1, rank))
    by_sender = group_dst.reshape(owners, edges)
    direct_hit = by_sender // pairs == my_owner
    direct_row = jnp.max(jnp.where(direct_hit, by_sender % pairs + 1, 0), axis=1)
    mirror_local = mirror - group_base
    turned_hit = by_sender[:, :, None] == mirror_local[None, None, :]
    turned_row = jnp.max(
        jnp.where(turned_hit, lax.iota(jnp.int32, pairs)[None, None, :] + 1, 0), axis=(1, 2)
    )
    direct_row = jnp.where(direct_row == 0, pairs, direct_row - 1)
    turned_row = jnp.where(turned_row == 0, pairs, turned_row - 1)

    owner_step = 8
    sent, own_half = call(
        sum_kernel,
        "sum",
        4,
        owners // owner_step,
        [
            blocks(owner_step, rank, rank),
            whole(pairs, half, rank),
            whole(pairs, half, rank),
        ],
        [whole(owners, half, rank), whole(pairs, half, rank)],
        [
            jax.ShapeDtypeStruct((owners, half, rank), BF16),
            jax.ShapeDtypeStruct((pairs, half, rank), BF16),
        ],
        4 * owners * rank**2,
        (2 * owners + 2 * pairs) * tile_bytes,
        [pltpu.VMEM((pairs + 1, half, rank), F32), pltpu.VMEM((pairs + 1, half, rank), F32)],
    )(direct_row, turned_row, mirror_owner, shift, arrived, base, amp_half)
    returned = exchange(sent)
    return call(
        join_kernel,
        "join",
        2,
        pairs // pair_step,
        [whole(owners, half, rank), blocks(pair_step, half, rank)],
        blocks(pair_step, rank, rank),
        jax.ShapeDtypeStruct((pairs, rank, rank), BF16),
        pairs * rank**2,
        (owners // 2 + 2 * pairs) * tile_bytes,
    )(lead, mirror_owner, returned, own_half)


def solution(mesh):
    in_specs = (
        P(("grp", "own"), None, None),
        P(("grp", "own"), None, None),
        P(("grp", "own"), None),
        P(),
        P(None, ("grp", "own")),
        P(("grp", "own")),
        P(("grp", "own")),
        P("grp"),
        P(("grp", "own")),
        P(("grp", "own"), None, None),
    )
    out_specs = P(("grp", "own"), None, None)
    return jax.shard_map(local, mesh=mesh, in_specs=in_specs, out_specs=out_specs, check_vma=False)
```

```python
import jax
import jax.numpy as jnp
from jax import lax
from jax.experimental import pallas as pl
from jax.experimental.pallas import tpu as pltpu
from jax.sharding import PartitionSpec as P

LANES = 128
F32 = jnp.float32
BF16 = jnp.bfloat16
KERNEL_VMEM = 16 * 2**20


def contract_last(left, right):
    return lax.dot_general(left, right, (((1,), (1,)), ((), ())), preferred_element_type=F32)


def project_kernel(src_ref, margin_ref, amps_ref, out_ref):
    def body(e, carry):
        tile = amps_ref[src_ref[e]]
        out_ref[e] = jnp.dot(margin_ref[e], tile, preferred_element_type=F32).astype(BF16)
        return carry

    lax.fori_loop(0, margin_ref.shape[0], body, 0, unroll=8)


def energy_kernel(amps_ref, ints_ref, out_ref):
    def body(p, carry):
        amp = amps_ref[p].astype(F32)
        integral = ints_ref[p].astype(F32)
        out_ref[p] = jnp.sum((2.0 * integral - integral.T) * amp, axis=0, keepdims=True)
        return carry

    lax.fori_loop(0, amps_ref.shape[0], body, 0, unroll=4)


def couple_kernel(table_ref, place_ref, owner_ref, fock_ref, proj_ref, margin_ref, out_ref, tiles, sems):
    half = margin_ref.shape[1] // 2
    edges = margin_ref.shape[0]

    def copies(e, other):
        direct = pltpu.make_async_copy(
            tiles.at[e, pl.ds(0, half)], out_ref.at[owner_ref[e], pl.ds(0, half)], sems.at[e, 0]
        )
        turned = pltpu.make_async_copy(
            tiles.at[e, pl.ds(half, half)], out_ref.at[other, pl.ds(half, half)], sems.at[e, 1]
        )
        return direct, turned

    def body(e, carry):
        code = table_ref[place_ref[e]]
        lead = (code & 1) == 1
        proj = proj_ref[e]
        marg = margin_ref[e]
        turned = jnp.concatenate([marg[half:], marg[:half]], axis=0)
        left = jnp.where(lead, proj, turned)
        right = jnp.where(lead, marg, proj)
        tiles[e] = (contract_last(left, right) * fock_ref[e]).astype(BF16)
        for copy in copies(e, code >> 1):
            copy.start()
        return carry

    lax.fori_loop(0, edges, body, 0, unroll=8)

    def finish(e, carry):
        for copy in copies(e, 0):
            copy.wait()
        return carry

    lax.fori_loop(0, edges, finish, 0, unroll=8)


def sum_kernel(direct_ref, turned_ref, target_ref, arrived_ref, sent_ref, own_ref, mark_ref, acc, tiles, sems, own_sem):
    half = arrived_ref.shape[1] // 2
    pairs = own_ref.shape[0]
    mark_ref[...] = jnp.zeros_like(mark_ref)
    acc[...] = jnp.zeros_like(acc)

    def body(s, carry):
        acc[direct_ref[s]] += arrived_ref[s, :half, :].astype(F32)
        acc[turned_ref[s]] += arrived_ref[s, half:, :].astype(F32)
        return carry

    lax.fori_loop(0, arrived_ref.shape[0], body, 0, unroll=4)

    def copy(p):
        return pltpu.make_async_copy(tiles.at[p], sent_ref.at[target_ref[p]], sems.at[p])

    def send(p, carry):
        tiles[p] = acc[p].astype(BF16)
        copy(p).start()
        return carry

    lax.fori_loop(0, pairs, send, 0, unroll=4)
    keep = pltpu.make_async_copy(acc.at[pl.ds(0, pairs)], own_ref, own_sem)
    keep.start()

    def finish(p, carry):
        copy(p).wait()
        return carry

    lax.fori_loop(0, pairs, finish, 0, unroll=4)
    keep.wait()


def local_kernel(fock_ref, amps_ref, ints_ref, pno_ref, out_ref):
    rank = amps_ref.shape[1]

    def body(p, carry):
        row = jnp.broadcast_to(pno_ref[p], (rank, rank))
        level = row + row.T - fock_ref[p]
        out_ref[p] = ints_ref[p].astype(F32) + 2.0 * level * amps_ref[p].astype(F32)
        return carry

    lax.fori_loop(0, amps_ref.shape[0], body, 0, unroll=4)


def join_kernel(lead_ref, target_ref, shift_ref, returned_ref, own_ref, local_ref, amps_ref, out_ref, tiles, results, in_sems, out_sems):
    pairs, half, _ = own_ref.shape

    def fetch(p):
        return pltpu.make_async_copy(returned_ref.at[target_ref[p]], tiles.at[p], in_sems.at[p])

    def store(p):
        return pltpu.make_async_copy(results.at[p], out_ref.at[p], out_sems.at[p])

    def start(p, carry):
        fetch(p).start()
        return carry

    def body(p, carry):
        fetch(p).wait()
        own = own_ref[p]
        other = tiles[p].astype(F32)
        rest = local_ref[p] - (2.0 * shift_ref[p]) * amps_ref[p].astype(F32)

        @pl.when(lead_ref[p] == 1)
        def _():
            results[p, :half, :] = (rest[:half] + own).astype(BF16)
            results[p, half:, :] = (rest[half:] + other).astype(BF16)

        @pl.when(lead_ref[p] == 0)
        def _():
            both = jnp.concatenate([other, own], axis=0).T
            results[p] = (rest + both).astype(BF16)

        store(p).start()
        return carry

    def finish(p, carry):
        store(p).wait()
        return carry

    lax.fori_loop(0, pairs, start, 0, unroll=4)
    lax.fori_loop(0, pairs, body, 0, unroll=2)
    lax.fori_loop(0, pairs, finish, 0, unroll=4)


SMEM = pl.BlockSpec(memory_space=pltpu.SMEM)
VMEM = pl.BlockSpec(memory_space=pltpu.VMEM)
HBM = pl.BlockSpec(memory_space=pltpu.HBM)


def call(kernel, name, scalars, arrays, out_shape, out_specs, flops, nbytes, scratch=(), specs=None):
    return pl.pallas_call(
        kernel,
        in_specs=[SMEM] * len(scalars) + (specs or [VMEM] * len(arrays)),
        out_specs=out_specs,
        out_shape=out_shape,
        scratch_shapes=scratch,
        name=name,
        cost_estimate=pl.CostEstimate(flops=flops, bytes_accessed=nbytes, transcendentals=0),
        compiler_params=pltpu.CompilerParams(vmem_limit_bytes=KERNEL_VMEM),
    )(*scalars, *arrays)


def pick_rows(lookup, hit_mask):
    return jnp.sum(jnp.where(hit_mask, lookup[None, :], 0.0), axis=1)


def swapped(value, axis, step):
    members = lax.axis_size(axis)
    return lax.ppermute(value, axis, [(i, i ^ step) for i in range(members)])


def all_sum(value, axis, steps):
    for step in steps:
        value = value + swapped(value, axis, step)
    return value


def powers(stop):
    return [1 << k for k in range(stop.bit_length() - 1)]


def exchange(tiles):
    return lax.all_to_all(tiles, "own", split_axis=0, concat_axis=0, tiled=True)


def local(
    amps, ints, pno_energy, occ_energy, pair_occ, mirror, edge_src, edge_dst, edge_fock, margin
):
    owners = lax.axis_size("own")
    groups = lax.axis_size("grp")
    my_owner = lax.axis_index("own")
    group_index = lax.axis_index("grp")
    pairs, rank, _ = amps.shape
    half = rank // 2
    edges = edge_src.shape[0]
    occ_count = occ_energy.shape[0]
    group_base = group_index * (owners * pairs)
    device_base = group_base + my_owner * pairs
    tile_bytes = rank * rank * 2

    ids = device_base + lax.iota(jnp.int32, pairs)
    lead = ((ids < mirror) ^ ((ids + mirror) % 2 == 1)).astype(jnp.int32)
    mirror_owner = (mirror - group_base) // pairs
    code = jnp.pad(mirror_owner * 2 + lead, (0, LANES - pairs))
    codes = exchange(jnp.broadcast_to(code[None, None, :], (owners, 1, LANES)))
    table = codes.reshape(owners * LANES)

    projected = call(
        project_kernel,
        "project",
        [edge_src - device_base],
        [margin, amps],
        jax.ShapeDtypeStruct((edges, rank, rank), BF16),
        VMEM,
        2 * edges * rank**3,
        (2 * edges + pairs) * tile_bytes,
    )

    group_dst = edge_dst - group_base
    dst_owner = group_dst // pairs
    dst_slot = group_dst % pairs
    my_owner_row = lax.dynamic_slice_in_dim(dst_owner, my_owner * edges, edges)
    my_slot_row = lax.dynamic_slice_in_dim(dst_slot, my_owner * edges, edges)
    outgoing = call(
        couple_kernel,
        "couple",
        [table, my_owner_row * LANES + my_slot_row, my_owner_row, edge_fock],
        [projected, margin],
        pltpu.HBM((owners, rank, rank), BF16),
        HBM,
        2 * edges * rank**3,
        (2 * edges + owners) * tile_bytes,
        [pltpu.VMEM((edges, rank, rank), BF16), pltpu.SemaphoreType.DMA((edges, 2))],
    )
    arrived = exchange(outgoing)

    lane_energy = call(
        energy_kernel,
        "energy",
        [],
        [amps, ints],
        jax.ShapeDtypeStruct((pairs, 1, rank), F32),
        VMEM,
        6 * pairs * rank**2,
        2 * pairs * tile_bytes,
    )
    pair_energy = jnp.sum(lane_energy, axis=(1, 2))
    padded = -(-occ_count // LANES) * LANES
    occ_ids = lax.iota(jnp.int32, padded)
    first_hit = pair_occ[0][:, None] == occ_ids[None, :]
    second_hit = pair_occ[1][:, None] == occ_ids[None, :]
    partial_value = jnp.sum(jnp.where(first_hit, pair_energy[:, None], 0.0), axis=0)
    total = partial_value.reshape(padded // LANES, LANES)
    own_steps = powers(owners)
    total = all_sum(total, "grp", powers(groups))
    total = all_sum(total, "own", own_steps[:-2])
    occ_wide = jnp.pad(occ_energy, (0, padded - occ_count))
    fock_pair = pick_rows(occ_wide, first_hit) + pick_rows(occ_wide, second_hit)

    by_sender = group_dst.reshape(owners, edges)
    direct_hit = by_sender // pairs == my_owner
    direct_row = jnp.max(jnp.where(direct_hit, by_sender % pairs + 1, 0), axis=1)
    mirror_local = mirror - group_base
    turned_hit = by_sender[:, :, None] == mirror_local[None, None, :]
    turned_row = jnp.max(
        jnp.where(turned_hit, lax.iota(jnp.int32, pairs)[None, None, :] + 1, 0), axis=(1, 2)
    )
    direct_row = jnp.where(direct_row == 0, pairs, direct_row - 1)
    turned_row = jnp.where(turned_row == 0, pairs, turned_row - 1)

    total, direct_row = lax.optimization_barrier((total, direct_row))

    sent, own_sum, mark = call(
        sum_kernel,
        "sum",
        [direct_row, turned_row, mirror_owner],
        [arrived],
        [
            pltpu.HBM((owners, half, rank), BF16),
            pltpu.HBM((pairs, half, rank), F32),
            jax.ShapeDtypeStruct((8, LANES), F32),
        ],
        [HBM, HBM, VMEM],
        4 * owners * rank**2,
        (2 * owners + 2 * pairs) * tile_bytes,
        [
            pltpu.VMEM((pairs + 1, half, rank), F32),
            pltpu.VMEM((pairs, half, rank), BF16),
            pltpu.SemaphoreType.DMA((pairs,)),
            pltpu.SemaphoreType.DMA,
        ],
    )
    total, fock_pair, mark = lax.optimization_barrier((total, fock_pair, mark))
    returned = exchange(sent)

    low, high = own_steps[-2:]
    moved = [swapped(total, "own", step) for step in (low, high, low + high)]
    total = total + moved[0] + (moved[1] + moved[2])
    occ_sums = total.reshape(padded)
    shift = 0.5 * (pick_rows(occ_sums, first_hit) + pick_rows(occ_sums, second_hit))
    twice_local = call(
        local_kernel,
        "local",
        [fock_pair],
        [amps, ints, pno_energy.reshape(pairs, 1, rank)],
        jax.ShapeDtypeStruct((pairs, rank, rank), F32),
        VMEM,
        6 * pairs * rank**2,
        4 * pairs * tile_bytes,
    )
    return call(
        join_kernel,
        "join",
        [lead, mirror_owner, shift],
        [returned, own_sum, twice_local, amps],
        pltpu.HBM((pairs, rank, rank), BF16),
        HBM,
        pairs * rank**2,
        (owners // 2 + 2 * pairs) * tile_bytes,
        [
            pltpu.VMEM((pairs, half, rank), BF16),
            pltpu.VMEM((pairs, rank, rank), BF16),
            pltpu.SemaphoreType.DMA((pairs,)),
            pltpu.SemaphoreType.DMA((pairs,)),
        ],
        [HBM, VMEM, VMEM, VMEM],
    )


def solution(mesh):
    in_specs = (
        P(("grp", "own"), None, None),
        P(("grp", "own"), None, None),
        P(("grp", "own"), None),
        P(),
        P(None, ("grp", "own")),
        P(("grp", "own")),
        P(("grp", "own")),
        P("grp"),
        P(("grp", "own")),
        P(("grp", "own"), None, None),
    )
    out_specs = P(("grp", "own"), None, None)
    return jax.shard_map(local, mesh=mesh, in_specs=in_specs, out_specs=out_specs, check_vma=False)
```

```python
import functools

import jax
import jax.numpy as jnp
from jax import lax
from jax.experimental import pallas as pl
from jax.experimental.pallas import tpu as pltpu
from jax.sharding import PartitionSpec as P

LANES = 128
F32 = jnp.float32
BF16 = jnp.bfloat16
KERNEL_VMEM = 16 * 2**20


def contract_last(left, right):
    return lax.dot_general(left, right, (((1,), (1,)), ((), ())), preferred_element_type=F32)


def project_kernel(src_ref, margin_ref, amps_ref, out_ref):
    def body(e, carry):
        tile = amps_ref[src_ref[e]]
        out_ref[e] = jnp.dot(margin_ref[e], tile, preferred_element_type=F32).astype(BF16)
        return carry

    lax.fori_loop(0, margin_ref.shape[0], body, 0, unroll=8)


def energy_kernel(amps_ref, ints_ref, out_ref):
    def body(p, carry):
        amp = amps_ref[p].astype(F32)
        integral = ints_ref[p].astype(F32)
        out_ref[p] = jnp.sum((2.0 * integral - integral.T) * amp, axis=0, keepdims=True)
        return carry

    lax.fori_loop(0, amps_ref.shape[0], body, 0, unroll=4)


def leads(pair, other):
    return ((pair < other) ^ ((pair + other) % 2 == 1)).astype(jnp.int32)


def couple_kernel(pairs, base_ref, table_ref, place_ref, owner_ref, pair_ref, fock_ref, proj_ref, margin_ref, out_ref, tiles, sems):
    edges = tiles.shape[0]
    half = tiles.shape[1] // 2
    scale = -(-(1 << 20) // pairs)
    reach = pairs * out_ref.shape[0]
    assert all(x * scale >> 20 == x // pairs for x in range(reach)) and reach * scale < 2**31

    def copies(e, other):
        direct = pltpu.make_async_copy(
            tiles.at[e, pl.ds(0, half)], out_ref.at[owner_ref[e], pl.ds(0, half)], sems.at[e, 0]
        )
        turned = pltpu.make_async_copy(
            tiles.at[e, pl.ds(half, half)], out_ref.at[other, pl.ds(half, half)], sems.at[e, 1]
        )
        return direct, turned

    def start(e, carry):
        twin = table_ref[place_ref[e]]
        pair = pair_ref[e]
        lead = (((pair < twin).astype(jnp.int32) + pair + twin) & 1) == 1
        other = ((twin - base_ref[0]) * scale) >> 20
        proj = proj_ref[e]
        marg = margin_ref[e]
        turned = jnp.concatenate([marg[half:], marg[:half]], axis=0)
        left = jnp.where(lead, proj, turned)
        right = jnp.where(lead, marg, proj)
        tiles[e] = (contract_last(left, right) * fock_ref[e]).astype(BF16)
        for copy in copies(e, other):
            copy.start()
        return carry

    def finish(e, carry):
        for copy in copies(e, 0):
            copy.wait()
        return carry

    lax.fori_loop(0, edges, start, 0, unroll=8)
    lax.fori_loop(0, edges, finish, 0, unroll=8)


def sum_kernel(direct_ref, turned_ref, target_ref, arrived_ref, sent_ref, mark_ref, direct_acc, turned_acc, tiles, sems):
    half = arrived_ref.shape[1] // 2
    pairs = tiles.shape[0]
    mark_ref[...] = jnp.zeros_like(mark_ref)
    direct_acc[...] = jnp.zeros_like(direct_acc)
    turned_acc[...] = jnp.zeros_like(turned_acc)

    def body(s, carry):
        direct_acc[direct_ref[s]] += arrived_ref[s, :half, :].astype(F32)
        turned_acc[turned_ref[s]] += arrived_ref[s, half:, :].astype(F32)
        return carry

    lax.fori_loop(0, arrived_ref.shape[0], body, 0, unroll=8)

    def copy(p):
        return pltpu.make_async_copy(tiles.at[p], sent_ref.at[target_ref[p]], sems.at[p])

    def send(p, carry):
        tiles[p] = (direct_acc[p] + turned_acc[p]).astype(BF16)
        copy(p).start()
        return carry

    def finish(p, carry):
        copy(p).wait()
        return carry

    lax.fori_loop(0, pairs, send, 0, unroll=4)
    lax.fori_loop(0, pairs, finish, 0, unroll=4)


def unit(rank):
    rows = lax.broadcasted_iota(jnp.int32, (rank, rank), 0)
    columns = lax.broadcasted_iota(jnp.int32, (rank, rank), 1)
    return (rows == columns).astype(F32).astype(BF16)


def local_kernel(lead_ref, target_ref, fock_ref, amps_ref, ints_ref, pno_ref, sent_ref, out_ref, mark_ref, results, sem):
    rank = amps_ref.shape[1]
    one = unit(rank)
    mark_ref[...] = jnp.zeros_like(mark_ref)

    def body(p, carry):
        row = jnp.broadcast_to(pno_ref[p], (rank, rank))
        level = row + row.T - fock_ref[p]
        twice = ints_ref[p].astype(F32) + 2.0 * level * amps_ref[p].astype(F32)
        own = sent_ref[target_ref[p]]
        none = jnp.zeros_like(own)
        upper = jnp.concatenate([own, none], axis=0).astype(F32)
        right = contract_last(one, jnp.concatenate([none, own], axis=0))
        results[p] = twice + jnp.where(lead_ref[p] == 1, upper, right)
        return carry

    lax.fori_loop(0, amps_ref.shape[0], body, 0, unroll=4)
    copy = pltpu.make_async_copy(results, out_ref, sem)
    copy.start()
    copy.wait()


def join_kernel(lead_ref, target_ref, shift_ref, returned_ref, local_ref, amps_ref, out_ref, tiles, locals_, results, sems, in_sems, out_sems):
    pairs, half, rank = tiles.shape
    chunks = in_sems.shape[0]
    count = pairs // chunks
    one = unit(rank)

    def fetch(p):
        return pltpu.make_async_copy(returned_ref.at[target_ref[p]], tiles.at[p], sems.at[p])

    def load(k):
        rows = pl.ds(k * count, count)
        return pltpu.make_async_copy(local_ref.at[rows], locals_.at[rows], in_sems.at[k])

    def store(k):
        rows = pl.ds(k * count, count)
        return pltpu.make_async_copy(results.at[rows], out_ref.at[rows], out_sems.at[k])

    for k in range(chunks):
        load(k).start()
        for p in range(k * count, (k + 1) * count):
            fetch(p).start()

    def body(k, carry):
        load(k).wait()
        for i in range(count):
            fetch(k * count + i).wait()
        for i in range(count):
            p = k * count + i
            other = tiles[p]
            none = jnp.zeros_like(other)
            lower = jnp.concatenate([none, other], axis=0).astype(F32)
            left = contract_last(one, jnp.concatenate([other, none], axis=0))
            rest = locals_[p] - (2.0 * shift_ref[p]) * amps_ref[p].astype(F32)
            results[p] = (rest + jnp.where(lead_ref[p] == 1, lower, left)).astype(BF16)
        store(k).start()
        return carry

    lax.fori_loop(0, chunks, body, 0)
    for k in range(chunks):
        store(k).wait()


SMEM = pl.BlockSpec(memory_space=pltpu.SMEM)
VMEM = pl.BlockSpec(memory_space=pltpu.VMEM)
HBM = pl.BlockSpec(memory_space=pltpu.HBM)


def call(kernel, name, scalars, arrays, out_shape, out_specs, flops, nbytes, scratch=(), specs=None):
    return pl.pallas_call(
        kernel,
        in_specs=[SMEM] * len(scalars) + (specs or [VMEM] * len(arrays)),
        out_specs=out_specs,
        out_shape=out_shape,
        scratch_shapes=scratch,
        name=name,
        cost_estimate=pl.CostEstimate(flops=flops, bytes_accessed=nbytes, transcendentals=0),
        compiler_params=pltpu.CompilerParams(vmem_limit_bytes=KERNEL_VMEM),
    )(*scalars, *arrays)


def pick_rows(lookup, hit_mask):
    return jnp.sum(jnp.where(hit_mask, lookup[None, :], 0.0), axis=1)


def swapped(value, axis, step):
    members = lax.axis_size(axis)
    return lax.ppermute(value, axis, [(i, i ^ step) for i in range(members)])


def all_sum(value, axis, steps):
    for step in steps:
        value = value + swapped(value, axis, step)
    return value


def powers(stop):
    return [1 << k for k in range(stop.bit_length() - 1)]


def exchange(tiles):
    return lax.all_to_all(tiles, "own", split_axis=0, concat_axis=0, tiled=True)


def local(
    amps, ints, pno_energy, occ_energy, pair_occ, mirror, edge_src, edge_dst, edge_fock, margin
):
    owners = lax.axis_size("own")
    groups = lax.axis_size("grp")
    my_owner = lax.axis_index("own")
    group_index = lax.axis_index("grp")
    pairs, rank, _ = amps.shape
    half = rank // 2
    edges = edge_src.shape[0]
    occ_count = occ_energy.shape[0]
    group_base = group_index * (owners * pairs)
    device_base = group_base + my_owner * pairs
    tile_bytes = rank * rank * 2

    ids = device_base + lax.iota(jnp.int32, pairs)
    lead = leads(ids, mirror)
    mirror_owner = (mirror - group_base) // pairs
    rows = jnp.broadcast_to(mirror[None, None, :], (owners, 1, pairs))
    rows = jnp.pad(rows, ((0, 0), (0, 0), (0, LANES - pairs)))
    table = exchange(rows).reshape(owners * LANES)

    projected = call(
        project_kernel,
        "project",
        [edge_src - device_base],
        [margin, amps],
        jax.ShapeDtypeStruct((edges, rank, rank), BF16),
        VMEM,
        2 * edges * rank**3,
        (2 * edges + pairs) * tile_bytes,
    )

    group_dst = edge_dst - group_base
    dst_owner = group_dst // pairs
    dst_slot = group_dst % pairs
    my_pair_row = lax.dynamic_slice_in_dim(edge_dst, my_owner * edges, edges)
    my_owner_row = lax.dynamic_slice_in_dim(dst_owner, my_owner * edges, edges)
    my_slot_row = lax.dynamic_slice_in_dim(dst_slot, my_owner * edges, edges)
    outgoing = call(
        functools.partial(couple_kernel, pairs),
        "couple",
        [group_base.reshape(1), table, my_owner_row * LANES + my_slot_row, my_owner_row, my_pair_row, edge_fock],
        [projected, margin],
        pltpu.HBM((owners, rank, rank), BF16),
        HBM,
        2 * edges * rank**3,
        3 * edges * tile_bytes,
        [pltpu.VMEM((edges, rank, rank), BF16), pltpu.SemaphoreType.DMA((edges, 2))],
    )
    arrived = exchange(outgoing)

    lane_energy = call(
        energy_kernel,
        "energy",
        [],
        [amps, ints],
        jax.ShapeDtypeStruct((pairs, 1, rank), F32),
        VMEM,
        6 * pairs * rank**2,
        2 * pairs * tile_bytes,
    )
    pair_energy = jnp.sum(lane_energy, axis=(1, 2))
    padded = -(-occ_count // LANES) * LANES
    occ_ids = lax.iota(jnp.int32, padded)
    first_hit = pair_occ[0][:, None] == occ_ids[None, :]
    second_hit = pair_occ[1][:, None] == occ_ids[None, :]
    partial_value = jnp.sum(jnp.where(first_hit, pair_energy[:, None], 0.0), axis=0)
    total = partial_value.reshape(padded // LANES, LANES)
    own_steps = powers(owners)
    total = all_sum(total, "grp", powers(groups))
    total = all_sum(total, "own", own_steps[:-2])
    occ_wide = jnp.pad(occ_energy, (0, padded - occ_count))
    fock_pair = pick_rows(occ_wide, first_hit) + pick_rows(occ_wide, second_hit)

    by_sender = group_dst.reshape(owners, edges)
    direct_hit = by_sender // pairs == my_owner
    direct_row = jnp.max(jnp.where(direct_hit, by_sender % pairs + 1, 0), axis=1)
    mirror_local = mirror - group_base
    turned_hit = by_sender[:, :, None] == mirror_local[None, None, :]
    turned_row = jnp.max(
        jnp.where(turned_hit, lax.iota(jnp.int32, pairs)[None, None, :] + 1, 0), axis=(1, 2)
    )
    direct_row = jnp.where(direct_row == 0, pairs, direct_row - 1)
    turned_row = jnp.where(turned_row == 0, pairs, turned_row - 1)

    total, direct_row = lax.optimization_barrier((total, direct_row))

    sent, mark = call(
        sum_kernel,
        "sum",
        [direct_row, turned_row, mirror_owner],
        [arrived],
        [pltpu.HBM((owners, half, rank), BF16), jax.ShapeDtypeStruct((8, LANES), F32)],
        [HBM, VMEM],
        4 * owners * rank**2,
        (owners + pairs) * tile_bytes,
        [
            pltpu.VMEM((pairs + 1, half, rank), F32),
            pltpu.VMEM((pairs + 1, half, rank), F32),
            pltpu.VMEM((pairs, half, rank), BF16),
            pltpu.SemaphoreType.DMA((pairs,)),
        ],
    )
    fock_pair = fock_pair + mark[0, 0]
    returned = exchange(sent)

    twice_local, done = call(
        local_kernel,
        "local",
        [lead, mirror_owner, fock_pair],
        [amps, ints, pno_energy.reshape(pairs, 1, rank), sent],
        [pltpu.HBM((pairs, rank, rank), F32), jax.ShapeDtypeStruct((8, LANES), F32)],
        [HBM, VMEM],
        6 * pairs * rank**2,
        4 * pairs * tile_bytes,
        [pltpu.VMEM((pairs, rank, rank), F32), pltpu.SemaphoreType.DMA],
    )
    total = total + done
    low, high = own_steps[-2:]
    moved = [swapped(total, "own", step) for step in (low, high, low + high)]
    total = total + moved[0] + (moved[1] + moved[2])
    occ_sums = total.reshape(padded)
    shift = 0.5 * (pick_rows(occ_sums, first_hit) + pick_rows(occ_sums, second_hit))
    return call(
        join_kernel,
        "join",
        [lead, mirror_owner, shift],
        [
            pltpu.with_memory_space_constraint(returned, pltpu.HBM),
            pltpu.with_memory_space_constraint(twice_local, pltpu.HBM),
            amps,
        ],
        pltpu.HBM((pairs, rank, rank), BF16),
        HBM,
        pairs * rank**2,
        (owners // 2 + 2 * pairs) * tile_bytes,
        [
            pltpu.VMEM((pairs, half, rank), BF16),
            pltpu.VMEM((pairs, rank, rank), F32),
            pltpu.VMEM((pairs, rank, rank), BF16),
            pltpu.SemaphoreType.DMA((pairs,)),
            pltpu.SemaphoreType.DMA((7,)),
            pltpu.SemaphoreType.DMA((7,)),
        ],
        [HBM, HBM, VMEM],
    )


def solution(mesh):
    in_specs = (
        P(("grp", "own"), None, None),
        P(("grp", "own"), None, None),
        P(("grp", "own"), None),
        P(),
        P(None, ("grp", "own")),
        P(("grp", "own")),
        P(("grp", "own")),
        P("grp"),
        P(("grp", "own")),
        P(("grp", "own"), None, None),
    )
    out_specs = P(("grp", "own"), None, None)
    return jax.shard_map(local, mesh=mesh, in_specs=in_specs, out_specs=out_specs, check_vma=False)
```

```python
import functools

import jax
import jax.numpy as jnp
from jax import lax
from jax.experimental import pallas as pl
from jax.experimental.pallas import tpu as pltpu
from jax.sharding import PartitionSpec as P

LANES = 128
F32 = jnp.float32
BF16 = jnp.bfloat16
KERNEL_VMEM = 16 * 2**20


def contract_last(left, right):
    return lax.dot_general(left, right, (((1,), (1,)), ((), ())), preferred_element_type=F32)


def project_kernel(src_ref, margin_ref, amps_ref, out_ref, margins, tiles, margin_sems, tile_sems):
    edges, pairs = margins.shape[0], tiles.shape[0]
    chunks = margin_sems.shape[0]
    count = edges // chunks
    base = (lax.axis_index("grp") * lax.axis_size("own") + lax.axis_index("own")) * pairs

    def load(k):
        rows = pl.ds(k * count, count)
        return pltpu.make_async_copy(margin_ref.at[rows], margins.at[rows], margin_sems.at[k])

    every = pltpu.make_async_copy(amps_ref, tiles, tile_sems)
    every.start()
    for k in range(chunks):
        load(k).start()
    every.wait()

    def body(k, carry):
        load(k).wait()
        for i in range(count):
            e = k * count + i
            tile = tiles[src_ref[e] - base]
            out_ref[e] = jnp.dot(margins[e], tile, preferred_element_type=F32).astype(BF16)
        return carry

    lax.fori_loop(0, chunks, body, 0)


def energy_kernel(amps_ref, ints_ref, out_ref):
    def body(p, carry):
        amp = amps_ref[p].astype(F32)
        integral = ints_ref[p].astype(F32)
        out_ref[p] = jnp.sum((2.0 * integral - integral.T) * amp, axis=0, keepdims=True)
        return carry

    lax.fori_loop(0, amps_ref.shape[0], body, 0, unroll=4)


def leads(pair, other):
    return ((pair < other) ^ ((pair + other) % 2 == 1)).astype(jnp.int32)


def couple_kernel(pairs, table_ref, dst_ref, fock_ref, proj_ref, margin_ref, out_ref, slots, sem):
    edges = proj_ref.shape[0]
    half = proj_ref.shape[1] // 2
    scale = -(-(1 << 20) // pairs)
    owners = out_ref.shape[0]
    reach = pairs * owners
    base = lax.axis_index("grp") * reach
    first = lax.axis_index("own") * edges
    assert all(x * scale >> 20 == x // pairs for x in range(reach)) and reach * scale < 2**31

    def place(e, carry):
        pair = dst_ref[first + e]
        owner = ((pair - base) * scale) >> 20
        twin = table_ref[owner * LANES + (pair - base - owner * pairs)]
        lead = (((pair < twin).astype(jnp.int32) + pair + twin) & 1) == 1
        other = ((twin - base) * scale) >> 20
        proj = proj_ref[e]
        marg = margin_ref[e]
        turned = jnp.concatenate([marg[half:], marg[:half]], axis=0)
        left = jnp.where(lead, proj, turned)
        right = jnp.where(lead, marg, proj)
        tile = (contract_last(left, right) * fock_ref[e]).astype(BF16)
        slots[owner, :half, :] = tile[:half]
        slots[other, half:, :] = tile[half:]
        return carry

    lax.fori_loop(0, edges, place, 0, unroll=8)
    copy = pltpu.make_async_copy(slots, out_ref, sem)
    copy.start()
    copy.wait()


def sum_kernel(direct_ref, turned_ref, target_ref, arrived_ref, sent_ref, mark_ref, direct_acc, turned_acc, tiles, sems):
    half = arrived_ref.shape[1] // 2
    pairs = tiles.shape[0]
    mark_ref[...] = jnp.zeros_like(mark_ref)
    direct_acc[...] = jnp.zeros_like(direct_acc)
    turned_acc[...] = jnp.zeros_like(turned_acc)

    def body(s, carry):
        direct_acc[direct_ref[s]] += arrived_ref[s, :half, :].astype(F32)
        turned_acc[turned_ref[s]] += arrived_ref[s, half:, :].astype(F32)
        return carry

    lax.fori_loop(0, arrived_ref.shape[0], body, 0, unroll=8)

    def copy(p):
        return pltpu.make_async_copy(tiles.at[p], sent_ref.at[target_ref[p]], sems.at[p])

    def send(p, carry):
        tiles[p] = (direct_acc[p] + turned_acc[p]).astype(BF16)
        copy(p).start()
        return carry

    def finish(p, carry):
        copy(p).wait()
        return carry

    lax.fori_loop(0, pairs, send, 0, unroll=4)
    lax.fori_loop(0, pairs, finish, 0, unroll=4)


def unit(rank):
    rows = lax.broadcasted_iota(jnp.int32, (rank, rank), 0)
    columns = lax.broadcasted_iota(jnp.int32, (rank, rank), 1)
    return (rows == columns).astype(F32).astype(BF16)


def local_kernel(lead_ref, target_ref, fock_ref, amps_ref, ints_ref, pno_ref, sent_ref, out_ref, mark_ref, results, sem):
    rank = amps_ref.shape[1]
    one = unit(rank)
    mark_ref[...] = jnp.zeros_like(mark_ref)

    def body(p, carry):
        row = jnp.broadcast_to(pno_ref[p], (rank, rank))
        level = row + row.T - fock_ref[p]
        twice = ints_ref[p].astype(F32) + 2.0 * level * amps_ref[p].astype(F32)
        own = sent_ref[target_ref[p]]
        none = jnp.zeros_like(own)
        upper = jnp.concatenate([own, none], axis=0).astype(F32)
        right = contract_last(one, jnp.concatenate([none, own], axis=0))
        results[p] = twice + jnp.where(lead_ref[p] == 1, upper, right)
        return carry

    lax.fori_loop(0, amps_ref.shape[0], body, 0, unroll=4)
    copy = pltpu.make_async_copy(results, out_ref, sem)
    copy.start()
    copy.wait()


def join_kernel(lead_ref, target_ref, shift_ref, returned_ref, local_ref, amps_ref, out_ref, tiles, locals_, results, sems, in_sems, out_sems):
    pairs, half, rank = tiles.shape
    chunks = in_sems.shape[0]
    count = pairs // chunks
    one = unit(rank)

    def fetch(p):
        return pltpu.make_async_copy(returned_ref.at[target_ref[p]], tiles.at[p], sems.at[p])

    def load(k):
        rows = pl.ds(k * count, count)
        return pltpu.make_async_copy(local_ref.at[rows], locals_.at[rows], in_sems.at[k])

    def store(k):
        rows = pl.ds(k * count, count)
        return pltpu.make_async_copy(results.at[rows], out_ref.at[rows], out_sems.at[k])

    for k in range(chunks):
        load(k).start()
        for p in range(k * count, (k + 1) * count):
            fetch(p).start()

    def body(k, carry):
        load(k).wait()
        for i in range(count):
            fetch(k * count + i).wait()
        for i in range(count):
            p = k * count + i
            other = tiles[p]
            none = jnp.zeros_like(other)
            lower = jnp.concatenate([none, other], axis=0).astype(F32)
            left = contract_last(one, jnp.concatenate([other, none], axis=0))
            rest = locals_[p] - (2.0 * shift_ref[p]) * amps_ref[p].astype(F32)
            results[p] = (rest + jnp.where(lead_ref[p] == 1, lower, left)).astype(BF16)
        store(k).start()
        return carry

    lax.fori_loop(0, chunks, body, 0)
    for k in range(chunks):
        store(k).wait()


SMEM = pl.BlockSpec(memory_space=pltpu.SMEM)
VMEM = pl.BlockSpec(memory_space=pltpu.VMEM)
HBM = pl.BlockSpec(memory_space=pltpu.HBM)


def call(kernel, name, scalars, arrays, out_shape, out_specs, flops, nbytes, scratch=(), specs=None):
    return pl.pallas_call(
        kernel,
        in_specs=[SMEM] * len(scalars) + (specs or [VMEM] * len(arrays)),
        out_specs=out_specs,
        out_shape=out_shape,
        scratch_shapes=scratch,
        name=name,
        cost_estimate=pl.CostEstimate(flops=flops, bytes_accessed=nbytes, transcendentals=0),
        compiler_params=pltpu.CompilerParams(vmem_limit_bytes=KERNEL_VMEM),
    )(*scalars, *arrays)


def pick_rows(lookup, hit_mask):
    return jnp.sum(jnp.where(hit_mask, lookup[None, :], 0.0), axis=1)


def swapped(value, axis, step):
    members = lax.axis_size(axis)
    return lax.ppermute(value, axis, [(i, i ^ step) for i in range(members)])


def all_sum(value, axis, steps):
    for step in steps:
        value = value + swapped(value, axis, step)
    return value


def powers(stop):
    return [1 << k for k in range(stop.bit_length() - 1)]


def exchange(tiles):
    return lax.all_to_all(tiles, "own", split_axis=0, concat_axis=0, tiled=True)


def local(
    amps, ints, pno_energy, occ_energy, pair_occ, mirror, edge_src, edge_dst, edge_fock, margin
):
    owners = lax.axis_size("own")
    groups = lax.axis_size("grp")
    my_owner = lax.axis_index("own")
    group_index = lax.axis_index("grp")
    pairs, rank, _ = amps.shape
    half = rank // 2
    edges = edge_src.shape[0]
    occ_count = occ_energy.shape[0]
    group_base = group_index * (owners * pairs)
    device_base = group_base + my_owner * pairs
    tile_bytes = rank * rank * 2

    ids = device_base + lax.iota(jnp.int32, pairs)
    lead = leads(ids, mirror)
    mirror_owner = (mirror - group_base) // pairs
    rows = jnp.broadcast_to(mirror[None, None, :], (owners, 1, pairs))
    rows = jnp.pad(rows, ((0, 0), (0, 0), (0, LANES - pairs)))
    table = exchange(rows).reshape(owners * LANES)

    projected = call(
        project_kernel,
        "project",
        [edge_src],
        [
            pltpu.with_memory_space_constraint(margin, pltpu.HBM),
            pltpu.with_memory_space_constraint(amps, pltpu.HBM),
        ],
        jax.ShapeDtypeStruct((edges, rank, rank), BF16),
        VMEM,
        2 * edges * rank**3,
        (2 * edges + pairs) * tile_bytes,
        [
            pltpu.VMEM((edges, rank, rank), BF16),
            pltpu.VMEM((pairs, rank, rank), BF16),
            pltpu.SemaphoreType.DMA((6,)),
            pltpu.SemaphoreType.DMA,
        ],
        [HBM, HBM],
    )

    group_dst = edge_dst - group_base
    outgoing = call(
        functools.partial(couple_kernel, pairs),
        "couple",
        [table, edge_dst, edge_fock],
        [projected, margin],
        pltpu.HBM((owners, rank, rank), BF16),
        HBM,
        2 * edges * rank**3,
        3 * edges * tile_bytes,
        [pltpu.VMEM((owners, rank, rank), BF16), pltpu.SemaphoreType.DMA],
    )
    arrived = exchange(outgoing)

    lane_energy = call(
        energy_kernel,
        "energy",
        [],
        [amps, ints],
        jax.ShapeDtypeStruct((pairs, 1, rank), F32),
        VMEM,
        6 * pairs * rank**2,
        2 * pairs * tile_bytes,
    )
    pair_energy = jnp.sum(lane_energy, axis=(1, 2))
    padded = -(-occ_count // LANES) * LANES
    occ_ids = lax.iota(jnp.int32, padded)
    first_hit = pair_occ[0][:, None] == occ_ids[None, :]
    second_hit = pair_occ[1][:, None] == occ_ids[None, :]
    partial_value = jnp.sum(jnp.where(first_hit, pair_energy[:, None], 0.0), axis=0)
    total = partial_value.reshape(padded // LANES, LANES)
    own_steps = powers(owners)
    total = all_sum(total, "grp", powers(groups))
    total = all_sum(total, "own", own_steps[:-2])
    occ_wide = jnp.pad(occ_energy, (0, padded - occ_count))
    fock_pair = pick_rows(occ_wide, first_hit) + pick_rows(occ_wide, second_hit)

    by_sender = group_dst.reshape(owners, edges)
    direct_hit = by_sender // pairs == my_owner
    direct_row = jnp.max(jnp.where(direct_hit, by_sender % pairs + 1, 0), axis=1)
    mirror_local = mirror - group_base
    turned_hit = by_sender[:, :, None] == mirror_local[None, None, :]
    turned_row = jnp.max(
        jnp.where(turned_hit, lax.iota(jnp.int32, pairs)[None, None, :] + 1, 0), axis=(1, 2)
    )
    direct_row = jnp.where(direct_row == 0, pairs, direct_row - 1)
    turned_row = jnp.where(turned_row == 0, pairs, turned_row - 1)

    total, direct_row = lax.optimization_barrier((total, direct_row))

    sent, mark = call(
        sum_kernel,
        "sum",
        [direct_row, turned_row, mirror_owner],
        [arrived],
        [pltpu.HBM((owners, half, rank), BF16), jax.ShapeDtypeStruct((8, LANES), F32)],
        [HBM, VMEM],
        4 * owners * rank**2,
        (owners + pairs) * tile_bytes,
        [
            pltpu.VMEM((pairs + 1, half, rank), F32),
            pltpu.VMEM((pairs + 1, half, rank), F32),
            pltpu.VMEM((pairs, half, rank), BF16),
            pltpu.SemaphoreType.DMA((pairs,)),
        ],
    )
    fock_pair = fock_pair + mark[0, 0]
    returned = exchange(sent)

    twice_local, done = call(
        local_kernel,
        "local",
        [lead, mirror_owner, fock_pair],
        [amps, ints, pno_energy.reshape(pairs, 1, rank), sent],
        [pltpu.HBM((pairs, rank, rank), F32), jax.ShapeDtypeStruct((8, LANES), F32)],
        [HBM, VMEM],
        6 * pairs * rank**2,
        4 * pairs * tile_bytes,
        [pltpu.VMEM((pairs, rank, rank), F32), pltpu.SemaphoreType.DMA],
    )
    total = total + done
    low, high = own_steps[-2:]
    moved = [swapped(total, "own", step) for step in (low, high, low + high)]
    total = total + moved[0] + (moved[1] + moved[2])
    occ_sums = total.reshape(padded)
    shift = 0.5 * (pick_rows(occ_sums, first_hit) + pick_rows(occ_sums, second_hit))
    return call(
        join_kernel,
        "join",
        [lead, mirror_owner, shift],
        [
            pltpu.with_memory_space_constraint(returned, pltpu.HBM),
            pltpu.with_memory_space_constraint(twice_local, pltpu.HBM),
            amps,
        ],
        pltpu.HBM((pairs, rank, rank), BF16),
        HBM,
        pairs * rank**2,
        (owners // 2 + 2 * pairs) * tile_bytes,
        [
            pltpu.VMEM((pairs, half, rank), BF16),
            pltpu.VMEM((pairs, rank, rank), F32),
            pltpu.VMEM((pairs, rank, rank), BF16),
            pltpu.SemaphoreType.DMA((pairs,)),
            pltpu.SemaphoreType.DMA((7,)),
            pltpu.SemaphoreType.DMA((7,)),
        ],
        [HBM, HBM, VMEM],
    )


def solution(mesh):
    in_specs = (
        P(("grp", "own"), None, None),
        P(("grp", "own"), None, None),
        P(("grp", "own"), None),
        P(),
        P(None, ("grp", "own")),
        P(("grp", "own")),
        P(("grp", "own")),
        P("grp"),
        P(("grp", "own")),
        P(("grp", "own"), None, None),
    )
    out_specs = P(("grp", "own"), None, None)
    return jax.shard_map(local, mesh=mesh, in_specs=in_specs, out_specs=out_specs, check_vma=False)
```

```python
import functools

import jax
import jax.numpy as jnp
from jax import lax
from jax.experimental import pallas as pl
from jax.experimental.pallas import tpu as pltpu
from jax.sharding import PartitionSpec as P

LANES = 128
F32 = jnp.float32
BF16 = jnp.bfloat16
KERNEL_VMEM = 16 * 2**20


def contract_last(left, right):
    return lax.dot_general(left, right, (((1,), (1,)), ((), ())), preferred_element_type=F32)


def project_kernel(src_ref, margin_ref, amps_ref, out_ref, margins, tiles, margin_sems, tile_sems):
    edges, pairs = margins.shape[0], tiles.shape[0]
    chunks = margin_sems.shape[0]
    count = edges // chunks
    base = (lax.axis_index("grp") * lax.axis_size("own") + lax.axis_index("own")) * pairs

    def load(k):
        rows = pl.ds(k * count, count)
        return pltpu.make_async_copy(margin_ref.at[rows], margins.at[rows], margin_sems.at[k])

    every = pltpu.make_async_copy(amps_ref, tiles, tile_sems)
    every.start()
    for k in range(chunks):
        load(k).start()
    every.wait()

    def body(k, carry):
        load(k).wait()
        for i in range(count):
            e = k * count + i
            tile = tiles[src_ref[e] - base]
            out_ref[e] = jnp.dot(margins[e], tile, preferred_element_type=F32).astype(BF16)
        return carry

    lax.fori_loop(0, chunks, body, 0)


def energy_kernel(amps_ref, ints_ref, out_ref):
    def body(p, carry):
        amp = amps_ref[p].astype(F32)
        integral = ints_ref[p].astype(F32)
        out_ref[p] = jnp.sum((2.0 * integral - integral.T) * amp, axis=0, keepdims=True)
        return carry

    lax.fori_loop(0, amps_ref.shape[0], body, 0, unroll=4)


def leads(pair, other):
    return ((pair < other) ^ ((pair + other) % 2 == 1)).astype(jnp.int32)


def couple_kernel(pairs, table_ref, dst_ref, fock_ref, proj_ref, margin_ref, out_ref, slots, sem):
    edges = proj_ref.shape[0]
    half = proj_ref.shape[1] // 2
    scale = -(-(1 << 20) // pairs)
    owners = out_ref.shape[0]
    reach = pairs * owners
    base = lax.axis_index("grp") * reach
    first = lax.axis_index("own") * edges
    assert all(x * scale >> 20 == x // pairs for x in range(reach)) and reach * scale < 2**31

    def place(e, carry):
        pair = dst_ref[first + e]
        owner = ((pair - base) * scale) >> 20
        twin = table_ref[owner * LANES + (pair - base - owner * pairs)]
        lead = (((pair < twin).astype(jnp.int32) + pair + twin) & 1) == 1
        other = ((twin - base) * scale) >> 20
        proj = proj_ref[e]
        marg = margin_ref[e]
        turned = jnp.concatenate([marg[half:], marg[:half]], axis=0)
        left = jnp.where(lead, proj, turned)
        right = jnp.where(lead, marg, proj)
        tile = (contract_last(left, right) * fock_ref[e]).astype(BF16)
        slots[owner, :half, :] = tile[:half]
        slots[other, half:, :] = tile[half:]
        return carry

    lax.fori_loop(0, edges, place, 0, unroll=8)
    copy = pltpu.make_async_copy(slots, out_ref, sem)
    copy.start()
    copy.wait()


def sum_kernel(direct_ref, turned_ref, target_ref, arrived_ref, sent_ref, mark_ref, direct_acc, turned_acc, tiles, sems):
    half = arrived_ref.shape[1] // 2
    pairs = tiles.shape[0]
    mark_ref[...] = jnp.zeros_like(mark_ref)
    direct_acc[...] = jnp.zeros_like(direct_acc)
    turned_acc[...] = jnp.zeros_like(turned_acc)

    def body(s, carry):
        direct_acc[direct_ref[s]] += arrived_ref[s, :half, :].astype(F32)
        turned_acc[turned_ref[s]] += arrived_ref[s, half:, :].astype(F32)
        return carry

    lax.fori_loop(0, arrived_ref.shape[0], body, 0, unroll=8)

    def copy(p):
        return pltpu.make_async_copy(tiles.at[p], sent_ref.at[target_ref[p]], sems.at[p])

    def send(p, carry):
        tiles[p] = (direct_acc[p] + turned_acc[p]).astype(BF16)
        copy(p).start()
        return carry

    def finish(p, carry):
        copy(p).wait()
        return carry

    lax.fori_loop(0, pairs, send, 0, unroll=4)
    lax.fori_loop(0, pairs, finish, 0, unroll=4)


def unit(rank):
    rows = lax.broadcasted_iota(jnp.int32, (rank, rank), 0)
    columns = lax.broadcasted_iota(jnp.int32, (rank, rank), 1)
    return (rows == columns).astype(F32).astype(BF16)


def local_kernel(lead_ref, target_ref, fock_ref, amps_ref, ints_ref, pno_ref, sent_ref, out_ref, mark_ref, results, sem):
    rank = amps_ref.shape[1]
    one = unit(rank)
    mark_ref[...] = jnp.zeros_like(mark_ref)

    def body(p, carry):
        row = jnp.broadcast_to(pno_ref[p], (rank, rank))
        level = row + row.T - fock_ref[p]
        twice = ints_ref[p].astype(F32) + 2.0 * level * amps_ref[p].astype(F32)
        own = sent_ref[target_ref[p]]
        none = jnp.zeros_like(own)
        upper = jnp.concatenate([own, none], axis=0).astype(F32)
        right = contract_last(one, jnp.concatenate([none, own], axis=0))
        results[p] = twice + jnp.where(lead_ref[p] == 1, upper, right)
        return carry

    lax.fori_loop(0, amps_ref.shape[0], body, 0, unroll=4)
    copy = pltpu.make_async_copy(results, out_ref, sem)
    copy.start()
    copy.wait()


def join_kernel(lead_ref, target_ref, shift_ref, returned_ref, local_ref, amps_ref, out_ref, tiles, locals_, results, sems, in_sems, out_sems):
    pairs, _, rank = tiles.shape
    chunks = in_sems.shape[0]
    count = pairs // chunks
    one = unit(rank)

    def fetch(p):
        return pltpu.make_async_copy(returned_ref.at[target_ref[p]], tiles.at[p], sems.at[p])

    def load(k):
        rows = pl.ds(k * count, count)
        return pltpu.make_async_copy(local_ref.at[rows], locals_.at[rows], in_sems.at[k])

    def store(k):
        rows = pl.ds(k * count, count)
        return pltpu.make_async_copy(results.at[rows], out_ref.at[rows], out_sems.at[k])

    for k in range(chunks):
        load(k).start()
        for p in range(k * count, (k + 1) * count):
            fetch(p).start()

    def body(k, carry):
        load(k).wait()
        for i in range(count):
            fetch(k * count + i).wait()
        for i in range(count):
            p = k * count + i
            other = tiles[p]
            none = jnp.zeros_like(other)
            lower = jnp.concatenate([none, other], axis=0).astype(F32)
            left = contract_last(one, jnp.concatenate([other, none], axis=0))
            rest = locals_[p] - (2.0 * shift_ref[p]) * amps_ref[p].astype(F32)
            results[p] = (rest + jnp.where(lead_ref[p] == 1, lower, left)).astype(BF16)
        store(k).start()
        return carry

    lax.fori_loop(0, chunks, body, 0)
    for k in range(chunks):
        store(k).wait()


SMEM = pl.BlockSpec(memory_space=pltpu.SMEM)
VMEM = pl.BlockSpec(memory_space=pltpu.VMEM)
HBM = pl.BlockSpec(memory_space=pltpu.HBM)


def call(kernel, scalars, arrays, out_shape, out_specs, flops, nbytes, scratch=(), specs=None):
    return pl.pallas_call(
        kernel,
        in_specs=[SMEM] * len(scalars) + (specs or [VMEM] * len(arrays)),
        out_specs=out_specs,
        out_shape=out_shape,
        scratch_shapes=scratch,
        cost_estimate=pl.CostEstimate(flops=flops, bytes_accessed=nbytes, transcendentals=0),
        compiler_params=pltpu.CompilerParams(vmem_limit_bytes=KERNEL_VMEM),
    )(*scalars, *arrays)


def pick_rows(lookup, hit_mask):
    return jnp.sum(jnp.where(hit_mask, lookup[None, :], 0.0), axis=1)


def swapped(value, axis, step):
    members = lax.axis_size(axis)
    return lax.ppermute(value, axis, [(i, i ^ step) for i in range(members)])


def all_sum(value, axis, steps):
    for step in steps:
        value = value + swapped(value, axis, step)
    return value


def powers(stop):
    return [1 << k for k in range(stop.bit_length() - 1)]


def exchange(tiles):
    return lax.all_to_all(tiles, "own", split_axis=0, concat_axis=0, tiled=True)


def local_part(
    amps, ints, pno_energy, occ_energy, pair_occ, mirror, edge_src, edge_dst, edge_fock, margin
):
    owners = lax.axis_size("own")
    groups = lax.axis_size("grp")
    my_owner = lax.axis_index("own")
    group_index = lax.axis_index("grp")
    pairs, rank, _ = amps.shape
    half = rank // 2
    edges = edge_src.shape[0]
    occ_count = occ_energy.shape[0]
    group_base = group_index * (owners * pairs)
    device_base = group_base + my_owner * pairs
    tile_bytes = rank * rank * 2

    ids = device_base + lax.iota(jnp.int32, pairs)
    lead = leads(ids, mirror)
    mirror_owner = (mirror - group_base) // pairs
    rows = jnp.broadcast_to(mirror[None, None, :], (owners, 1, pairs))
    rows = jnp.pad(rows, ((0, 0), (0, 0), (0, LANES - pairs)))
    table = exchange(rows).reshape(owners * LANES)

    projected = call(
        project_kernel,
        [edge_src],
        [
            pltpu.with_memory_space_constraint(margin, pltpu.HBM),
            pltpu.with_memory_space_constraint(amps, pltpu.HBM),
        ],
        jax.ShapeDtypeStruct((edges, rank, rank), BF16),
        VMEM,
        2 * edges * rank**3,
        (2 * edges + pairs) * tile_bytes,
        [
            pltpu.VMEM((edges, rank, rank), BF16),
            pltpu.VMEM((pairs, rank, rank), BF16),
            pltpu.SemaphoreType.DMA((6,)),
            pltpu.SemaphoreType.DMA,
        ],
        [HBM, HBM],
    )

    group_dst = edge_dst - group_base
    outgoing = call(
        functools.partial(couple_kernel, pairs),
        [table, edge_dst, edge_fock],
        [projected, margin],
        pltpu.HBM((owners, rank, rank), BF16),
        HBM,
        2 * edges * rank**3,
        3 * edges * tile_bytes,
        [pltpu.VMEM((owners, rank, rank), BF16), pltpu.SemaphoreType.DMA],
    )
    arrived = exchange(outgoing)

    lane_energy = call(
        energy_kernel,
        [],
        [amps, ints],
        jax.ShapeDtypeStruct((pairs, 1, rank), F32),
        VMEM,
        6 * pairs * rank**2,
        2 * pairs * tile_bytes,
    )
    pair_energy = jnp.sum(lane_energy, axis=(1, 2))
    padded = -(-occ_count // LANES) * LANES
    occ_ids = lax.iota(jnp.int32, padded)
    first_hit = pair_occ[0][:, None] == occ_ids[None, :]
    second_hit = pair_occ[1][:, None] == occ_ids[None, :]
    partial_value = jnp.sum(jnp.where(first_hit, pair_energy[:, None], 0.0), axis=0)
    total = partial_value.reshape(padded // LANES, LANES)
    own_steps = powers(owners)
    total = all_sum(total, "grp", powers(groups))
    total = all_sum(total, "own", own_steps[:-3])
    late = swapped(total, "own", own_steps[-3])
    occ_wide = jnp.pad(occ_energy, (0, padded - occ_count))
    fock_pair = pick_rows(occ_wide, first_hit) + pick_rows(occ_wide, second_hit)

    by_sender = group_dst.reshape(owners, edges)
    direct_hit = by_sender // pairs == my_owner
    direct_row = jnp.max(jnp.where(direct_hit, by_sender % pairs + 1, 0), axis=1)
    mirror_local = mirror - group_base
    turned_hit = by_sender[:, :, None] == mirror_local[None, None, :]
    turned_row = jnp.max(
        jnp.where(turned_hit, lax.iota(jnp.int32, pairs)[None, None, :] + 1, 0), axis=(1, 2)
    )
    direct_row = jnp.where(direct_row == 0, pairs, direct_row - 1)
    turned_row = jnp.where(turned_row == 0, pairs, turned_row - 1)


    sent, mark = call(
        sum_kernel,
        [direct_row, turned_row, mirror_owner],
        [arrived],
        [pltpu.HBM((owners, half, rank), BF16), jax.ShapeDtypeStruct((8, LANES), F32)],
        [HBM, VMEM],
        4 * owners * rank**2,
        (owners + pairs) * tile_bytes,
        [
            pltpu.VMEM((pairs + 1, half, rank), F32),
            pltpu.VMEM((pairs + 1, half, rank), F32),
            pltpu.VMEM((pairs, half, rank), BF16),
            pltpu.SemaphoreType.DMA((pairs,)),
        ],
    )
    fock_pair = fock_pair + mark[0, 0]
    returned = exchange(sent)

    twice_local, done = call(
        local_kernel,
        [lead, mirror_owner, fock_pair],
        [amps, ints, pno_energy.reshape(pairs, 1, rank), sent],
        [pltpu.HBM((pairs, rank, rank), F32), jax.ShapeDtypeStruct((8, LANES), F32)],
        [HBM, VMEM],
        6 * pairs * rank**2,
        4 * pairs * tile_bytes,
        [pltpu.VMEM((pairs, rank, rank), F32), pltpu.SemaphoreType.DMA],
    )
    total = total + late + done
    low, high = own_steps[-2:]
    moved = [swapped(total, "own", step) for step in (low, high, low + high)]
    total = total + moved[0] + (moved[1] + moved[2])
    occ_sums = total.reshape(padded)
    shift = 0.5 * (pick_rows(occ_sums, first_hit) + pick_rows(occ_sums, second_hit))
    return call(
        join_kernel,
        [lead, mirror_owner, shift],
        [
            pltpu.with_memory_space_constraint(returned, pltpu.HBM),
            pltpu.with_memory_space_constraint(twice_local, pltpu.HBM),
            amps,
        ],
        pltpu.HBM((pairs, rank, rank), BF16),
        HBM,
        pairs * rank**2,
        (owners // 2 + 2 * pairs) * tile_bytes,
        [
            pltpu.VMEM((pairs, half, rank), BF16),
            pltpu.VMEM((pairs, rank, rank), F32),
            pltpu.VMEM((pairs, rank, rank), BF16),
            pltpu.SemaphoreType.DMA((pairs,)),
            pltpu.SemaphoreType.DMA((4,)),
            pltpu.SemaphoreType.DMA((4,)),
        ],
        [HBM, HBM, VMEM],
    )


def solution(mesh):
    in_specs = (
        P(("grp", "own"), None, None),
        P(("grp", "own"), None, None),
        P(("grp", "own"), None),
        P(),
        P(None, ("grp", "own")),
        P(("grp", "own")),
        P(("grp", "own")),
        P("grp"),
        P(("grp", "own")),
        P(("grp", "own"), None, None),
    )
    out_specs = P(("grp", "own"), None, None)
    return jax.shard_map(local_part, mesh=mesh, in_specs=in_specs, out_specs=out_specs, check_vma=False)
```
